32 devices in a mesh: grp: 1, lat: 32 (over z, y, x, core).
Axes of the slice: x: 2, y: 2, z: 4, core: 2. Of those that a mesh axis runs over, the one named last changes fastest.
Arguments:
- fields: bfloat16 [768, 64, 2048], P(('grp', 'lat')), may hold values from -6 to 6
- spectral_weight: bfloat16 [2, 128, 64, 128], replicated, may hold values from -0.5 to 0.5
- local_weight: bfloat16 [2, 64, 64], replicated, may hold values from -0.75 to 0.75
Outputs:
- updated: bfloat16 [768, 64, 2048], P(('grp', 'lat'))
The draws below stay inside these ranges and needn't reach their ends.
All inputs are finite; a program needn't handle non-finite values.
Results may differ from the reference program's by a relative error of at most 0.011.
Values may be sent and summed in bfloat16 or wider, within the bound.
A program may use at most 128 MiB of HBM per device.

```python
import math
import jax
import jax.numpy as jnp

C = 64
NLON = 2048
KX = 128
KY = 128
LAYERS = 2
ROWS_DEV = 24
NLAT = 768


def levels(stream_key, extent, split, low, largest):
    level = 1.0
    for position, shards_of in split:
        heights = jax.random.uniform(jax.random.fold_in(jax.random.fold_in(stream_key, 6), position), (shards_of,), jnp.float32, low / len(split), largest / len(split))
        level = level * jnp.repeat(jnp.exp(heights), extent[position] // shards_of).reshape((-1,) + (1,) * (len(extent) - 1 - position))
    return level


def centred(own_key, dims, spread, reach, split=(), kind=jnp.bfloat16):
    result = jax.random.normal(own_key, dims, jnp.float32) * spread
    if len(split) > 0:
        result = levels(own_key, dims, split, -0.22, 0.18) * result
    return jnp.clip(result, min=-reach, max=reach).astype(kind)


def setup_inputs(seed: int = 0, part: int = 0) -> dict:
    streams_of = jax.random.split(jax.random.key(seed), 4)
    part_keys = jax.random.split(jax.random.fold_in(streams_of[3], part), 4)
    fields = centred(part_keys[0], (NLAT, C, NLON), 1.0, 6.0, ((0, 32),))
    spectral_weight = centred(streams_of[1], (LAYERS, KX, C, 2 * C), (2 * C) ** -0.5, 0.5)
    local_weight = centred(streams_of[2], (LAYERS, C, C), C ** -0.5, 0.75)
    return {"fields": fields, "spectral_weight": spectral_weight, "local_weight": local_weight}


def lon_forward_table(lon_count, mode_count):
    cells = jnp.arange(lon_count, dtype=jnp.int32)[:, None]
    modes = jnp.arange(mode_count, dtype=jnp.int32)[None, :]
    angle = 2.0 * jnp.pi / lon_count * (cells * modes % lon_count).astype(jnp.float32)
    factor = 1.0 / math.sqrt(lon_count)
    return jnp.stack([jnp.cos(angle) * factor, -jnp.sin(angle) * factor], axis=1).astype(jnp.bfloat16)

def lon_back_table(lon_count, mode_count):
    modes = jnp.arange(mode_count, dtype=jnp.int32)[:, None]
    cells = jnp.arange(lon_count, dtype=jnp.int32)[None, :]
    angle = 2.0 * jnp.pi / lon_count * (cells * modes % lon_count).astype(jnp.float32)
    factor = 1.0 / math.sqrt(mode_count)
    return jnp.stack([jnp.cos(angle) * factor, -jnp.sin(angle) * factor], axis=1).astype(jnp.bfloat16)

def kept_wavenumbers(lat_count, kept_count):
    index = jnp.arange(kept_count, dtype=jnp.int32)
    return jnp.where(index < kept_count // 2, index, lat_count - kept_count + index).astype(jnp.int32)

def row_latitudes(lat_count, block_rows):
    rowids = jnp.arange(lat_count, dtype=jnp.int32)
    stride = lat_count // block_rows
    return (rowids % block_rows * stride + rowids // block_rows).astype(jnp.int32)

def lat_tables(lat_count, kept_count, block_rows):
    waves = kept_wavenumbers(lat_count, kept_count)
    latitudes = row_latitudes(lat_count, block_rows)
    angle = 2.0 * jnp.pi / lat_count * (waves[:, None] * latitudes[None, :] % lat_count).astype(jnp.float32)
    forward = jnp.stack([jnp.cos(angle), jnp.sin(angle)], axis=0) * (1.0 / math.sqrt(lat_count))
    backward = jnp.stack([jnp.cos(angle).T, jnp.sin(angle).T], axis=0) * (1.0 / math.sqrt(kept_count))
    return (forward.astype(jnp.bfloat16), backward.astype(jnp.bfloat16))

def lat_forward(table, values, channels):
    products = jnp.einsum('pjn,nkc->pjkc', table.astype(jnp.float32), values.astype(jnp.float32))
    real_part = products[0, ..., :channels] + products[1, ..., channels:]
    imag_part = products[0, ..., channels:] - products[1, ..., :channels]
    return jnp.concatenate([real_part, imag_part], axis=-1)

def lat_backward(table, modes, channels):
    products = jnp.einsum('pnj,jkc->pnkc', table.astype(jnp.float32), modes.astype(jnp.float32))
    real_part = products[0, ..., :channels] - products[1, ..., channels:]
    imag_part = products[1, ..., :channels] + products[0, ..., channels:]
    return jnp.concatenate([real_part, imag_part], axis=-1)

def mix_matrix(weight, channels):
    real_w = weight[..., :channels]
    imag_w = weight[..., channels:]
    lower = jnp.concatenate([-imag_w, real_w], axis=-1)
    return jnp.concatenate([weight, lower], axis=1)

def reference(fields, spectral_weight, local_weight):
    forward_lon = lon_forward_table(NLON, KX).astype(jnp.float32)
    backward_lon = lon_back_table(NLON, KX).astype(jnp.float32)
    forward_lat, backward_lat = lat_tables(NLAT, KY, ROWS_DEV)
    current = fields
    for layer_idx in range(LAYERS):
        wide = current.astype(jnp.float32)
        lon_modes = jnp.einsum('rcl,lpk->rkpc', wide, forward_lon)
        lon_modes = lon_modes.reshape(NLAT, KX, 2 * C).astype(jnp.bfloat16)
        lat_modes = lat_forward(forward_lat, lon_modes, C).astype(jnp.bfloat16)
        mixing = mix_matrix(spectral_weight[layer_idx], C).astype(jnp.float32)
        mixed_modes = jnp.einsum('jkc,kcd->jkd', lat_modes.astype(jnp.float32), mixing).astype(jnp.bfloat16)
        lat_back = lat_backward(backward_lat, mixed_modes, C).astype(jnp.bfloat16)
        spectral = jnp.einsum('rkpc,kpl->rcl', lat_back.reshape(NLAT, KX, 2, C).astype(jnp.float32), backward_lon)
        pointwise = jnp.einsum('rcl,cd->rdl', wide, local_weight[layer_idx].astype(jnp.float32))
        current = jax.nn.gelu(spectral + pointwise, approximate=True).astype(jnp.bfloat16)
    return current
```

```python
import functools
import math

import jax
import jax.numpy as jnp
import numpy as np
from jax import lax
from jax.experimental import pallas as pl
from jax.experimental.pallas import tpu as pltpu
from jax.sharding import PartitionSpec as P

KY = 128
MESH = pl.DeviceIdType.MESH


def lon_table(lon_count, mode_count):
    cells = np.arange(lon_count, dtype=np.int64)[:, None]
    modes = np.arange(mode_count, dtype=np.int64)[None, :]
    angle = (2.0 * np.pi / lon_count) * (cells * modes % lon_count)
    return np.stack([np.cos(angle), -np.sin(angle)], axis=1)


def lat_tables(devices, group, row_count, kept):
    lat_count = devices * row_count
    outer = devices // group
    index = np.arange(kept, dtype=np.int64)
    waves = np.where(index < kept // 2, index, lat_count - kept + index)
    device = np.arange(outer)[:, None, None] * group + np.arange(group)[None, :, None]
    latitudes = (np.arange(row_count)[None, None, :] * devices + device).reshape(outer, -1)
    angle = (2.0 * np.pi / lat_count) * (waves[None, :, None] * latitudes[:, None, :] % lat_count)
    both = np.concatenate([np.cos(angle), np.sin(angle)], axis=1) / math.sqrt(lat_count)
    turned = angle.transpose(0, 2, 1)
    back = np.concatenate([np.cos(turned), np.sin(turned)], axis=1) / math.sqrt(kept)
    return both, back


def lat_kernel(
    group, outer, steps, rows, kept, channels,
    x_ref, mix_ref, fwd_ref, bwd_ref, y_ref,
    r_buf, p_buf, q_buf, m_buf, v_buf,
    local_sem, a_send, a_recv, b_send, b_recv, c_send, c_recv, d_send, d_recv,
):
    me = lax.axis_index("lat")
    z = me // group
    s = lax.rem(me, group)
    rows_all = rows * group

    def inner_peer(i):
        return lax.rem(s + i, group)

    def outer_peer(i):
        return lax.rem(z + i, outer)

    barrier = pltpu.get_barrier_semaphore()
    for i in range(1, group):
        pl.semaphore_signal(
            barrier, inc=1, device_id={"lat": z * group + inner_peer(i)}, device_id_type=MESH
        )
    for i in range(1, outer):
        pl.semaphore_signal(
            barrier, inc=1, device_id={"lat": outer_peer(i) * group + s}, device_id_type=MESH
        )

    def block(who):
        return pl.ds(pl.multiple_of(who * rows, 8), rows)

    def a_copy(t, i):
        to = inner_peer(i)
        return pltpu.make_async_remote_copy(
            src_ref=x_ref.at[pl.ds((to * steps + t) * outer, outer)],
            dst_ref=r_buf.at[t, :, block(s)],
            send_sem=a_send.at[t, i], recv_sem=a_recv.at[t, i],
            device_id={"lat": z * group + to}, device_id_type=MESH,
        )

    def b_copy(t, i):
        to = outer_peer(i)
        return pltpu.make_async_remote_copy(
            src_ref=p_buf.at[t, to], dst_ref=q_buf.at[t, z],
            send_sem=b_send.at[t, i], recv_sem=b_recv.at[t, i],
            device_id={"lat": to * group + s}, device_id_type=MESH,
        )

    def c_copy(t, i):
        to = outer_peer(i)
        return pltpu.make_async_remote_copy(
            src_ref=m_buf.at[t, z], dst_ref=m_buf.at[t, z],
            send_sem=c_send.at[t, i], recv_sem=c_recv.at[t, i],
            device_id={"lat": to * group + s}, device_id_type=MESH,
        )

    def d_copy(t, i):
        to = inner_peer(i)
        return pltpu.make_async_remote_copy(
            src_ref=v_buf.at[t, :, block(to)],
            dst_ref=y_ref.at[pl.ds((s * steps + t) * outer, outer)],
            send_sem=d_send.at[t, i], recv_sem=d_recv.at[t, i],
            device_id={"lat": z * group + to}, device_id_type=MESH,
        )

    def own_in(t):
        return pltpu.make_async_copy(
            x_ref.at[pl.ds((s * steps + t) * outer, outer)], r_buf.at[t, :, block(s)],
            local_sem.at[0, t],
        )

    def own_out(t):
        return pltpu.make_async_copy(
            v_buf.at[t, :, block(s)], y_ref.at[pl.ds((s * steps + t) * outer, outer)],
            local_sem.at[1, t],
        )

    for t in range(steps):
        own_in(t).start()
    pl.semaphore_wait(barrier, group - 1 + outer - 1)
    for t in range(steps):
        for i in range(1, group):
            a_copy(t, i).start()

    lane = lax.broadcasted_iota(jnp.int32, (1, 2 * channels), 1)
    fwd_sign = jnp.where(lane < channels, 1.0, -1.0).astype(jnp.float32)
    width = 2 * channels

    def forward(t):
        own_in(t).wait()
        for i in range(1, group):
            a_copy(t, i).wait_recv()
        for first in range(0, outer, 2):
            many = min(2, outer - first)
            pair = jnp.concatenate([r_buf[t, first + u] for u in range(many)], axis=1)
            both = jnp.dot(fwd_ref[...], pair, preferred_element_type=jnp.float32)
            for u in range(many):
                part = both[:, u * width:(u + 1) * width]
                out = part[:kept] + pltpu.roll(part[kept:], channels, 1) * fwd_sign
                p_buf[t, first + u] = out.astype(jnp.bfloat16)
        for i in range(1, outer):
            b_copy(t, i).start()

    def middle(t):
        total = p_buf[t, z].astype(jnp.float32)
        for i in range(1, outer):
            b_copy(t, i).wait_recv()
        for i in range(1, outer):
            total = total + q_buf[t, outer_peer(i)].astype(jnp.float32)
        mixed = jnp.dot(
            total.astype(jnp.bfloat16), mix_ref[t], preferred_element_type=jnp.float32
        )
        m_buf[t, z] = mixed.astype(jnp.bfloat16)
        for i in range(1, outer):
            c_copy(t, i).start()

    def backward(t):
        for i in range(1, outer):
            c_copy(t, i).wait_recv()
        for first in range(0, outer, 2):
            many = min(2, outer - first)
            pair = jnp.concatenate([m_buf[t, first + u] for u in range(many)], axis=1)
            both = jnp.dot(bwd_ref[...], pair, preferred_element_type=jnp.float32)
            for u in range(many):
                part = both[:, u * width:(u + 1) * width]
                out = part[:rows_all] - pltpu.roll(part[rows_all:], channels, 1) * fwd_sign
                v_buf[t, first + u] = out.astype(jnp.bfloat16)
        for i in range(1, group):
            d_copy(t, i).start()
        own_out(t).start()

    for step in range(steps + 2):
        if step < steps:
            forward(step)
        if 0 <= step - 1 < steps:
            middle(step - 1)
        if 0 <= step - 2 < steps:
            backward(step - 2)

    for t in range(steps):
        own_out(t).wait()
        for i in range(1, group):
            d_copy(t, i).wait()
            a_copy(t, i).wait_send()
        for i in range(1, outer):
            b_copy(t, i).wait_send()
            c_copy(t, i).wait_send()


def lat_part(x, mixing, forward_lat, backward_lat, devices, group):
    modes, rows, width = x.shape
    outer = devices // group
    steps = modes // devices
    kept = backward_lat.shape[1]
    dma = pltpu.SemaphoreType.DMA
    vmem = pl.BlockSpec(memory_space=pltpu.VMEM)
    return pl.pallas_call(
        functools.partial(lat_kernel, group, outer, steps, rows, kept, width // 2),
        out_shape=jax.ShapeDtypeStruct(x.shape, jnp.bfloat16),
        in_specs=[vmem] * 4,
        out_specs=vmem,
        scratch_shapes=[
            pltpu.VMEM((steps, outer, rows * group, width), jnp.bfloat16),
            pltpu.VMEM((steps, outer, kept, width), jnp.bfloat16),
            pltpu.VMEM((steps, outer, kept, width), jnp.bfloat16),
            pltpu.VMEM((steps, outer, kept, width), jnp.bfloat16),
            pltpu.VMEM((steps, outer, rows * group, width), jnp.bfloat16),
            dma((2, steps)),
            dma((steps, group)), dma((steps, group)),
            dma((steps, outer)), dma((steps, outer)),
            dma((steps, outer)), dma((steps, outer)),
            dma((steps, group)), dma((steps, group)),
        ],
        compiler_params=pltpu.CompilerParams(collective_id=0, has_side_effects=True),
        name="lat_part",
    )(x, mixing, forward_lat, backward_lat)


def mix_matrix(weight, channels):
    real_w = weight[..., :channels]
    imag_w = weight[..., channels:]
    lower = jnp.concatenate([-imag_w, real_w], axis=-1)
    return jnp.concatenate([weight, lower], axis=-2)


def shards(fields, spectral_weight, local_weight):
    row_count, channels, lon_count = fields.shape
    layer_count, mode_rows = spectral_weight.shape[:2]
    devices = lax.axis_size("lat")
    me = lax.axis_index("lat")
    group = math.gcd(devices, 8)
    outer = devices // group
    steps = mode_rows // devices
    table = lon_table(lon_count, mode_rows)
    forward_lon = jnp.asarray(table / math.sqrt(lon_count), jnp.bfloat16)
    backward_lon = jnp.asarray(
        table.transpose(2, 1, 0) / math.sqrt(mode_rows), jnp.bfloat16
    )
    forward_all, backward_all = lat_tables(devices, group, row_count, KY)
    forward_lat = lax.dynamic_index_in_dim(
        jnp.asarray(forward_all, jnp.bfloat16), me // group, 0, keepdims=False
    )
    backward_lat = lax.dynamic_index_in_dim(
        jnp.asarray(backward_all, jnp.bfloat16), me // group, 0, keepdims=False
    )
    grouped = spectral_weight.reshape(
        layer_count, group, steps, outer, channels, 2 * channels
    )
    grouped = lax.dynamic_index_in_dim(grouped, me % group, 1, keepdims=False)
    grouped = lax.dynamic_index_in_dim(grouped, me // group, 2, keepdims=False)
    mixing = mix_matrix(grouped, channels)
    current = fields
    for layer_idx in range(layer_count):
        x = jnp.einsum(
            "rcl,lpk->krpc", current, forward_lon, preferred_element_type=jnp.float32
        ).astype(jnp.bfloat16).reshape(mode_rows, row_count, 2 * channels)
        y = lat_part(x, mixing[layer_idx], forward_lat, backward_lat, devices, group)
        spectral = jnp.einsum(
            "krpc,kpl->rcl", y.reshape(mode_rows, row_count, 2, channels), backward_lon,
            preferred_element_type=jnp.float32,
        )
        pointwise = jnp.einsum(
            "rcl,cd->rdl", current, local_weight[layer_idx], preferred_element_type=jnp.float32
        )
        current = jax.nn.gelu(spectral + pointwise, approximate=True).astype(jnp.bfloat16)
    return current


def solution(mesh):
    return jax.shard_map(
        shards,
        mesh=mesh,
        in_specs=(P(("grp", "lat"), None, None), P(), P()),
        out_specs=P(("grp", "lat"), None, None),
        check_vma=False,
    )
```

```python
import functools
import math

import jax
import jax.numpy as jnp
import numpy as np
from jax import lax
from jax.experimental import pallas as pl
from jax.experimental.pallas import tpu as pltpu
from jax.sharding import PartitionSpec as P

KY = 128
MESH = pl.DeviceIdType.MESH
LAG = (0, 1, 2, 3, 4)
ROW_BLOCK = 8


def lon_table(lon_count, mode_count):
    cells = np.arange(lon_count, dtype=np.int64)[:, None]
    modes = np.arange(mode_count, dtype=np.int64)[None, :]
    angle = (2.0 * np.pi / lon_count) * (cells * modes % lon_count)
    return np.stack([np.cos(angle), -np.sin(angle)], axis=1)


def lat_tables(devices, group, row_count, kept):
    lat_count = devices * row_count
    outer = devices // group
    index = np.arange(kept, dtype=np.int64)
    waves = np.where(index < kept // 2, index, lat_count - kept + index)
    device = np.arange(outer)[:, None, None] * group + np.arange(group)[None, :, None]
    latitudes = (np.arange(row_count)[None, None, :] * devices + device).reshape(outer, -1)
    angle = (2.0 * np.pi / lat_count) * (waves[None, :, None] * latitudes[:, None, :] % lat_count)
    both = np.concatenate([np.cos(angle), np.sin(angle)], axis=1) / math.sqrt(lat_count)
    turned = angle.transpose(0, 2, 1)
    back = np.concatenate([np.cos(turned), np.sin(turned)], axis=1) / math.sqrt(kept)
    return both, back


def lat_kernel(
    group, outer, steps, rows, kept, channels,
    x_ref, mix_ref, fwd_ref, bwd_ref, y_ref,
    r_buf, p_buf, q_buf, m_buf, v_buf, fwd_buf, bwd_buf, f_buf, acc, f_sem, g_sem,
    local_sem, a_send, a_recv, b_send, b_recv, c_send, c_recv, d_send, d_recv,
):
    me = lax.axis_index("lat")
    z = me // group
    s = lax.rem(me, group)
    rows_all = rows * group

    def inner_peer(i):
        return lax.rem(s + i, group)

    def outer_peer(i):
        return lax.rem(z + i, outer)

    barrier = pltpu.get_barrier_semaphore()
    for i in range(1, group):
        pl.semaphore_signal(
            barrier, inc=1, device_id={"lat": z * group + inner_peer(i)}, device_id_type=MESH
        )
    for i in range(1, outer):
        pl.semaphore_signal(
            barrier, inc=1, device_id={"lat": outer_peer(i) * group + s}, device_id_type=MESH
        )

    def block(who):
        return pl.ds(pl.multiple_of(who * rows, 8), rows)

    def a_copy(t, i):
        to = inner_peer(i)
        return pltpu.make_async_remote_copy(
            src_ref=x_ref.at[pl.ds((to * steps + t) * outer, outer)],
            dst_ref=r_buf.at[t, :, block(s)],
            send_sem=a_send.at[t, i], recv_sem=a_recv.at[t, i],
            device_id={"lat": z * group + to}, device_id_type=MESH,
        )

    def b_copy(t, i):
        to = outer_peer(i)
        return pltpu.make_async_remote_copy(
            src_ref=p_buf.at[t, to], dst_ref=q_buf.at[t, z],
            send_sem=b_send.at[t, i], recv_sem=b_recv.at[t, i],
            device_id={"lat": to * group + s}, device_id_type=MESH,
        )

    def c_copy(t, i):
        to = outer_peer(i)
        return pltpu.make_async_remote_copy(
            src_ref=m_buf.at[t, z], dst_ref=m_buf.at[t, z],
            send_sem=c_send.at[t, i], recv_sem=c_recv.at[t, i],
            device_id={"lat": to * group + s}, device_id_type=MESH,
        )

    def d_copy(t, i):
        to = inner_peer(i)
        return pltpu.make_async_remote_copy(
            src_ref=v_buf.at[t, :, block(to)],
            dst_ref=y_ref.at[pl.ds((s * steps + t) * outer, outer)],
            send_sem=d_send.at[t, i], recv_sem=d_recv.at[t, i],
            device_id={"lat": z * group + to}, device_id_type=MESH,
        )

    def own_in(t):
        return pltpu.make_async_copy(
            x_ref.at[pl.ds((s * steps + t) * outer, outer)], r_buf.at[t, :, block(s)],
            local_sem.at[0, t],
        )

    def own_out(t):
        return pltpu.make_async_copy(
            v_buf.at[t, :, block(s)], y_ref.at[pl.ds((s * steps + t) * outer, outer)],
            local_sem.at[1, t],
        )

    def f_copy(t):
        return pltpu.make_async_remote_copy(
            src_ref=p_buf.at[t, outer - 1 - z], dst_ref=f_buf.at[t],
            send_sem=f_sem.at[0, t], recv_sem=f_sem.at[1, t],
            device_id={"lat": jnp.where(z == 0, 1, outer - 2) * group + s}, device_id_type=MESH,
        )

    def g_copy(t):
        block_of = outer_peer(2)
        return pltpu.make_async_remote_copy(
            src_ref=m_buf.at[t, block_of], dst_ref=m_buf.at[t, block_of],
            send_sem=g_sem.at[0, t], recv_sem=g_sem.at[1, t],
            device_id={"lat": (outer - 1 - block_of) * group + s}, device_id_type=MESH,
        )

    relay = outer == 4
    last = outer - 1
    at_end = jnp.logical_or(z == 0, z == last)
    inside = jnp.logical_not(at_end)

    fwd_copy = pltpu.make_async_copy(fwd_ref.at[z], fwd_buf, local_sem.at[0, steps])
    bwd_copy = pltpu.make_async_copy(bwd_ref.at[z], bwd_buf, local_sem.at[1, steps])
    fwd_copy.start()
    bwd_copy.start()
    for t in range(steps):
        own_in(t).start()
    pl.semaphore_wait(barrier, group - 1 + outer - 1)
    for t in range(steps):
        for i in range(1, group):
            a_copy(t, i).start()
    fwd_copy.wait()
    bwd_copy.wait()

    lane = lax.broadcasted_iota(jnp.int32, (1, 2 * channels), 1)
    fwd_sign = jnp.where(lane < channels, 1.0, -1.0).astype(jnp.float32)
    width = 2 * channels

    def forward(t):
        own_in(t).wait()
        for i in range(1, group):
            a_copy(t, i).wait_recv()
        for first in range(0, outer, 2):
            many = min(2, outer - first)
            pair = jnp.concatenate([r_buf[t, first + u] for u in range(many)], axis=1)
            both = jnp.dot(fwd_buf[...], pair, preferred_element_type=jnp.float32)
            for u in range(many):
                part = both[:, u * width:(u + 1) * width]
                out = part[:kept] + pltpu.roll(part[kept:], channels, 1) * fwd_sign
                p_buf[t, first + u] = out.astype(jnp.bfloat16)
        if not relay:
            for i in range(1, outer):
                b_copy(t, i).start()
            return
        pl.when(at_end)(lambda: f_copy(t).start())
        pl.when(at_end)(lambda: b_copy(t, 2).start())
        pl.when(z != last)(lambda: b_copy(t, 1).start())
        pl.when(z != 0)(lambda: b_copy(t, last).start())

    def relay_sum(t):
        if not relay:
            return

        @pl.when(inside)
        def _():
            f_copy(t).wait_recv()
            to = outer_peer(2)
            p_buf[t, to] = (
                p_buf[t, to].astype(jnp.float32) + f_buf[t].astype(jnp.float32)
            ).astype(jnp.bfloat16)
            b_copy(t, 2).start()

    def collect(t, i):
        b_copy(t, i).wait_recv()
        acc[...] += q_buf[t, lax.rem(z + outer - i, outer)].astype(jnp.float32)

    def middle(t):
        acc[...] = p_buf[t, z].astype(jnp.float32)
        if relay:
            pl.when(z != 0)(lambda: collect(t, 1))
            pl.when(z != last)(lambda: collect(t, last))
            collect(t, 2)
        else:
            for i in range(1, outer):
                collect(t, i)
        mixed = jnp.dot(
            acc[...].astype(jnp.bfloat16), mix_ref[t], preferred_element_type=jnp.float32
        )
        m_buf[t, z] = mixed.astype(jnp.bfloat16)
        if relay:
            c_copy(t, 2).start()
            pl.when(z != last)(lambda: c_copy(t, 1).start())
            pl.when(z != 0)(lambda: c_copy(t, last).start())
        else:
            for i in range(1, outer):
                c_copy(t, i).start()

    def relay_out(t):
        if not relay:
            return

        @pl.when(inside)
        def _():
            c_copy(t, 2).wait_recv()
            g_copy(t).start()

    def backward(t):
        if relay:
            pl.when(z != 0)(lambda: c_copy(t, 1).wait_recv())
            pl.when(z != last)(lambda: c_copy(t, last).wait_recv())
            pl.when(at_end)(lambda: c_copy(t, 2).wait_recv())
            pl.when(at_end)(lambda: g_copy(t).wait_recv())
        else:
            for i in range(1, outer):
                c_copy(t, i).wait_recv()
        for first in range(0, outer, 2):
            many = min(2, outer - first)
            pair = jnp.concatenate([m_buf[t, first + u] for u in range(many)], axis=1)
            both = jnp.dot(bwd_buf[...], pair, preferred_element_type=jnp.float32)
            for u in range(many):
                part = both[:, u * width:(u + 1) * width]
                out = part[:rows_all] - pltpu.roll(part[rows_all:], channels, 1) * fwd_sign
                v_buf[t, first + u] = out.astype(jnp.bfloat16)
        for i in range(1, group):
            d_copy(t, i).start()
        own_out(t).start()

    stages = tuple(zip((forward, relay_sum, middle, relay_out, backward), LAG))
    for step in range(steps + max(LAG)):
        for stage, lag in stages:
            if 0 <= step - lag < steps:
                stage(step - lag)

    for t in range(steps):
        own_out(t).wait()
        for i in range(1, group):
            d_copy(t, i).wait()
            a_copy(t, i).wait_send()
        if relay:
            pl.when(at_end)(lambda: f_copy(t).wait_send())
            pl.when(inside)(lambda: g_copy(t).wait_send())
            for copy in (b_copy, c_copy):
                copy(t, 2).wait_send()
                pl.when(z != last)(lambda: copy(t, 1).wait_send())
                pl.when(z != 0)(lambda: copy(t, last).wait_send())
        else:
            for i in range(1, outer):
                b_copy(t, i).wait_send()
                c_copy(t, i).wait_send()


def lat_part(x, mixing, forward_lat, backward_lat, devices, group):
    modes, rows, width = x.shape
    outer = devices // group
    steps = modes // devices
    kept = backward_lat.shape[2]
    dma = pltpu.SemaphoreType.DMA
    vmem = pl.BlockSpec(memory_space=pltpu.VMEM)
    hbm = pl.BlockSpec(memory_space=pl.ANY)
    return pl.pallas_call(
        functools.partial(lat_kernel, group, outer, steps, rows, kept, width // 2),
        out_shape=jax.ShapeDtypeStruct(x.shape, jnp.bfloat16),
        in_specs=[vmem, vmem, hbm, hbm],
        out_specs=vmem,
        scratch_shapes=[
            pltpu.VMEM((steps, outer, rows * group, width), jnp.bfloat16),
            pltpu.VMEM((steps, outer, kept, width), jnp.bfloat16),
            pltpu.VMEM((steps, outer, kept, width), jnp.bfloat16),
            pltpu.VMEM((steps, outer, kept, width), jnp.bfloat16),
            pltpu.VMEM((steps, outer, rows * group, width), jnp.bfloat16),
            pltpu.VMEM(forward_lat.shape[1:], jnp.bfloat16),
            pltpu.VMEM(backward_lat.shape[1:], jnp.bfloat16),
            pltpu.VMEM((steps, kept, width), jnp.bfloat16),
            pltpu.VMEM((kept, width), jnp.float32),
            dma((2, steps)), dma((2, steps)),
            dma((2, steps + 1)),
            dma((steps, group)), dma((steps, group)),
            dma((steps, outer)), dma((steps, outer)),
            dma((steps, outer)), dma((steps, outer)),
            dma((steps, group)), dma((steps, group)),
        ],
        compiler_params=pltpu.CompilerParams(collective_id=0, has_side_effects=True),
        name="lat_part",
    )(x, mixing, forward_lat, backward_lat)


def modes_out(flat, x_ref, turn):
    modes, rows, width = x_ref.shape
    channels = width // 2
    for n in range(rows):
        part = flat[n * channels:(n + 1) * channels]
        stacked = jnp.concatenate([part[:, :modes], part[:, modes:]], axis=0)
        turn[pl.ds(n, modes, stride=rows), :] = stacked.T
    x_ref[...] = turn[...].reshape(modes, rows, width).astype(jnp.bfloat16)


def lon_kernel(h_ref, table_ref, x_ref, turn):
    rows, channels, lon_count = h_ref.shape
    flat = jnp.dot(
        h_ref[...].reshape(rows * channels, lon_count), table_ref[...],
        preferred_element_type=jnp.float32,
    )
    modes_out(flat, x_ref, turn)


def field_kernel(with_modes, y_ref, h_ref, back_ref, local_ref, *rest):
    if with_modes:
        table_ref, out_ref, x_ref, turn, turned = rest
    else:
        out_ref, turn, turned = rest
    modes, rows, width = y_ref.shape
    channels = width // 2
    lon_count = h_ref.shape[2]
    span = local_ref.shape[0] // channels
    turn[...] = y_ref[...].astype(jnp.float32).reshape(modes * rows, width)
    for n in range(rows):
        across = turn[pl.ds(n, modes, stride=rows), :].T
        turned[n * channels:(n + 1) * channels] = jnp.concatenate(
            [across[:channels], across[channels:]], axis=1
        ).astype(jnp.bfloat16)
    chunk = min(512, lon_count)
    inner = math.sqrt(2.0 / math.pi)
    for first in range(0, rows, span):
        many = span * channels
        spectrum = turned[first * channels:first * channels + many]
        for column in range(0, lon_count, chunk):
            cells = slice(column, column + chunk)
            total = jnp.dot(
                spectrum, back_ref[:, cells], preferred_element_type=jnp.float32
            ) + jnp.dot(
                local_ref[...], h_ref[first:first + span, :, cells].reshape(many, chunk),
                preferred_element_type=jnp.float32,
            )
            curve = jnp.tanh(total * (inner + (inner * 0.044715) * (total * total)))
            out_ref[first:first + span, :, cells] = (
                (total * (0.5 + 0.5 * curve)).astype(jnp.bfloat16).reshape(span, channels, chunk)
            )
    if with_modes:
        flat = jnp.dot(
            out_ref[...].reshape(rows * channels, lon_count), table_ref[...],
            preferred_element_type=jnp.float32,
        )
        modes_out(flat, x_ref, turn)


def whole_block(array):
    return pl.BlockSpec(array.shape, lambda i: (0,) * array.ndim, pipeline_mode=pl.Buffered(1))


def lon_part(h, table):
    rows, channels, lon_count = h.shape
    modes = table.shape[1] // 2
    width = 2 * channels
    return pl.pallas_call(
        lon_kernel,
        grid=(rows // ROW_BLOCK,),
        out_shape=jax.ShapeDtypeStruct((modes, rows, width), jnp.bfloat16),
        in_specs=[
            pl.BlockSpec((ROW_BLOCK, channels, lon_count), lambda i: (i, 0, 0)),
            whole_block(table),
        ],
        out_specs=pl.BlockSpec((modes, ROW_BLOCK, width), lambda i: (0, i, 0)),
        scratch_shapes=[pltpu.VMEM((modes * ROW_BLOCK, width), jnp.float32)],
        name="lon_part",
    )(h, table)


def field_part(y, h, back, local, table=None):
    rows, channels, lon_count = h.shape
    modes, _, width = y.shape
    field = pl.BlockSpec((ROW_BLOCK, channels, lon_count), lambda i: (i, 0, 0))
    spectral = pl.BlockSpec((modes, ROW_BLOCK, width), lambda i: (0, i, 0))
    with_modes = table is not None
    operands = [y, h, back, local] + ([table] if with_modes else [])
    shapes = [jax.ShapeDtypeStruct(h.shape, jnp.bfloat16)]
    if with_modes:
        shapes.append(jax.ShapeDtypeStruct(y.shape, jnp.bfloat16))
    out = pl.pallas_call(
        functools.partial(field_kernel, with_modes),
        grid=(rows // ROW_BLOCK,),
        out_shape=shapes,
        in_specs=[spectral, field] + [whole_block(a) for a in operands[2:]],
        out_specs=[field, spectral][:len(shapes)],
        scratch_shapes=[
            pltpu.VMEM((modes * ROW_BLOCK, width), jnp.float32),
            pltpu.VMEM((ROW_BLOCK * channels, 2 * modes), jnp.bfloat16),
        ],
        name="field_part",
    )(*operands)
    return (out[0], out[1]) if with_modes else (out[0], None)


def mix_matrix(weight, channels):
    real_w = weight[..., :channels]
    imag_w = weight[..., channels:]
    lower = jnp.concatenate([-imag_w, real_w], axis=-1)
    return jnp.concatenate([weight, lower], axis=-2)


def shards(fields, spectral_weight, local_weight):
    row_count, channels, lon_count = fields.shape
    layer_count, mode_rows = spectral_weight.shape[:2]
    devices = lax.axis_size("lat")
    me = lax.axis_index("lat")
    group = math.gcd(devices, 8)
    outer = devices // group
    steps = mode_rows // devices
    table = lon_table(lon_count, mode_rows)
    forward_lon = jnp.asarray(
        (table / math.sqrt(lon_count)).reshape(lon_count, 2 * mode_rows), jnp.bfloat16
    )
    backward_lon = jnp.asarray(
        (table.transpose(1, 2, 0) / math.sqrt(mode_rows)).reshape(2 * mode_rows, lon_count),
        jnp.bfloat16,
    )
    span = max(1, min(ROW_BLOCK, 256 // channels))
    local = jnp.einsum(
        "ab,lcd->ladbc", jnp.eye(span, dtype=jnp.bfloat16), local_weight
    ).reshape(layer_count, span * channels, span * channels)
    forward_all, backward_all = lat_tables(devices, group, row_count, KY)
    forward_lat = jnp.asarray(forward_all, jnp.bfloat16)
    backward_lat = jnp.asarray(backward_all, jnp.bfloat16)
    grouped = spectral_weight.reshape(
        layer_count, group, steps, outer, channels, 2 * channels
    )
    grouped = lax.dynamic_index_in_dim(grouped, me % group, 1, keepdims=False)
    grouped = lax.dynamic_index_in_dim(grouped, me // group, 2, keepdims=False)
    mixing = mix_matrix(grouped, channels)
    current = fields
    x = lon_part(current, forward_lon)
    for layer_idx in range(layer_count):
        y = lat_part(x, mixing[layer_idx], forward_lat, backward_lat, devices, group)
        last_layer = layer_idx == layer_count - 1
        current, x = field_part(
            y, current, backward_lon, local[layer_idx], None if last_layer else forward_lon
        )
    return current


def solution(mesh):
    return jax.shard_map(
        shards,
        mesh=mesh,
        in_specs=(P(("grp", "lat"), None, None), P(), P()),
        out_specs=P(("grp", "lat"), None, None),
        check_vma=False,
    )
```

```python
import functools
import math

import jax
import jax.numpy as jnp
import numpy as np
from jax import lax
from jax.experimental import pallas as pl
from jax.experimental.pallas import tpu as pltpu
from jax.sharding import PartitionSpec as P

KY = 128
MESH = pl.DeviceIdType.MESH
LAG = (0, 1, 2, 3, 4)
ROW_BLOCK = 8
CHUNK = 512


def lon_table(lon_count, mode_count):
    cells = np.arange(lon_count, dtype=np.int64)[:, None]
    modes = np.arange(mode_count, dtype=np.int64)[None, :]
    angle = (2.0 * np.pi / lon_count) * (cells * modes % lon_count)
    return np.stack([np.cos(angle), -np.sin(angle)], axis=1)


def lat_tables(devices, group, row_count, kept):
    lat_count = devices * row_count
    outer = devices // group
    index = np.arange(kept, dtype=np.int64)
    waves = np.where(index < kept // 2, index, lat_count - kept + index)
    device = np.arange(outer)[:, None, None] * group + np.arange(group)[None, :, None]
    latitudes = (np.arange(row_count)[None, None, :] * devices + device).reshape(outer, -1)
    angle = (2.0 * np.pi / lat_count) * (waves[None, :, None] * latitudes[:, None, :] % lat_count)
    both = np.concatenate([np.cos(angle), np.sin(angle)], axis=1) / math.sqrt(lat_count)
    turned = angle.transpose(0, 2, 1)
    back = np.concatenate([np.cos(turned), np.sin(turned)], axis=1) / math.sqrt(kept)
    return both, back


def lat_kernel(
    layer, group, outer, steps, rows, kept, channels,
    x_ref, weight_ref, fwd_ref, bwd_ref, y_ref,
    r_buf, p_buf, q_buf, m_buf, v_buf, fwd_buf, bwd_buf, w_buf, mix_buf, f_buf, acc, f_sem, g_sem,
    local_sem, w_sem, a_send, a_recv, b_send, b_recv, c_send, c_recv, d_send, d_recv,
):
    me = lax.axis_index("lat")
    z = me // group
    s = lax.rem(me, group)
    rows_all = rows * group

    def inner_peer(i):
        return lax.rem(s + i, group)

    def outer_peer(i):
        return lax.rem(z + i, outer)

    barrier = pltpu.get_barrier_semaphore()
    for i in range(1, group):
        pl.semaphore_signal(
            barrier, inc=1, device_id={"lat": z * group + inner_peer(i)}, device_id_type=MESH
        )
    for i in range(1, outer):
        pl.semaphore_signal(
            barrier, inc=1, device_id={"lat": outer_peer(i) * group + s}, device_id_type=MESH
        )

    def block(who):
        return pl.ds(pl.multiple_of(who * rows, 8), rows)

    def a_copy(t, i):
        to = inner_peer(i)
        return pltpu.make_async_remote_copy(
            src_ref=x_ref.at[pl.ds((to * steps + t) * outer, outer)],
            dst_ref=r_buf.at[t, :, block(s)],
            send_sem=a_send.at[t, i], recv_sem=a_recv.at[t, i],
            device_id={"lat": z * group + to}, device_id_type=MESH,
        )

    def b_copy(t, i):
        to = outer_peer(i)
        return pltpu.make_async_remote_copy(
            src_ref=p_buf.at[t, to], dst_ref=q_buf.at[t, z],
            send_sem=b_send.at[t, i], recv_sem=b_recv.at[t, i],
            device_id={"lat": to * group + s}, device_id_type=MESH,
        )

    def c_copy(t, i):
        to = outer_peer(i)
        return pltpu.make_async_remote_copy(
            src_ref=m_buf.at[t, z], dst_ref=m_buf.at[t, z],
            send_sem=c_send.at[t, i], recv_sem=c_recv.at[t, i],
            device_id={"lat": to * group + s}, device_id_type=MESH,
        )

    def d_copy(t, i):
        to = inner_peer(i)
        return pltpu.make_async_remote_copy(
            src_ref=v_buf.at[t, :, block(to)],
            dst_ref=y_ref.at[pl.ds((s * steps + t) * outer, outer)],
            send_sem=d_send.at[t, i], recv_sem=d_recv.at[t, i],
            device_id={"lat": z * group + to}, device_id_type=MESH,
        )

    def own_in(t):
        return pltpu.make_async_copy(
            x_ref.at[pl.ds((s * steps + t) * outer, outer)], r_buf.at[t, :, block(s)],
            local_sem.at[0, t],
        )

    def own_out(t):
        return pltpu.make_async_copy(
            v_buf.at[t, :, block(s)], y_ref.at[pl.ds((s * steps + t) * outer, outer)],
            local_sem.at[1, t],
        )

    def f_copy(t):
        return pltpu.make_async_remote_copy(
            src_ref=p_buf.at[t, outer - 1 - z], dst_ref=f_buf.at[t],
            send_sem=f_sem.at[0, t], recv_sem=f_sem.at[1, t],
            device_id={"lat": jnp.where(z == 0, 1, outer - 2) * group + s}, device_id_type=MESH,
        )

    def g_copy(t):
        block_of = outer_peer(2)
        return pltpu.make_async_remote_copy(
            src_ref=m_buf.at[t, block_of], dst_ref=m_buf.at[t, block_of],
            send_sem=g_sem.at[0, t], recv_sem=g_sem.at[1, t],
            device_id={"lat": (outer - 1 - block_of) * group + s}, device_id_type=MESH,
        )

    relay = outer == 4
    last = outer - 1
    at_end = jnp.logical_or(z == 0, z == last)
    inside = jnp.logical_not(at_end)

    fwd_copy = pltpu.make_async_copy(fwd_ref.at[z], fwd_buf, local_sem.at[0, steps])
    bwd_copy = pltpu.make_async_copy(bwd_ref.at[z], bwd_buf, local_sem.at[1, steps])
    w_copies = [
        pltpu.make_async_copy(
            weight_ref.at[layer, (s * steps + t) * outer + z], w_buf.at[t], w_sem.at[t]
        )
        for t in range(steps)
    ]
    fwd_copy.start()
    bwd_copy.start()
    for copy in w_copies:
        copy.start()
    for t in range(steps):
        own_in(t).start()
    pl.semaphore_wait(barrier, group - 1 + outer - 1)
    for t in range(steps):
        for i in range(1, group):
            a_copy(t, i).start()
    fwd_copy.wait()
    bwd_copy.wait()

    lane = lax.broadcasted_iota(jnp.int32, (1, 2 * channels), 1)
    fwd_sign = jnp.where(lane < channels, 1.0, -1.0).astype(jnp.float32)
    width = 2 * channels
    for t in range(steps):
        w_copies[t].wait()
        weight = w_buf[t].astype(jnp.float32)
        mix_buf[t, :channels] = w_buf[t]
        mix_buf[t, channels:] = (
            pltpu.roll(weight, channels, 1) * -fwd_sign
        ).astype(jnp.bfloat16)

    def forward(t):
        own_in(t).wait()
        for i in range(1, group):
            a_copy(t, i).wait_recv()
        for first in range(0, outer, 2):
            many = min(2, outer - first)
            pair = jnp.concatenate([r_buf[t, first + u] for u in range(many)], axis=1)
            both = jnp.dot(fwd_buf[...], pair, preferred_element_type=jnp.float32)
            for u in range(many):
                part = both[:, u * width:(u + 1) * width]
                out = part[:kept] + pltpu.roll(part[kept:], channels, 1) * fwd_sign
                p_buf[t, first + u] = out.astype(jnp.bfloat16)
        if not relay:
            for i in range(1, outer):
                b_copy(t, i).start()
            return
        pl.when(at_end)(lambda: f_copy(t).start())
        pl.when(at_end)(lambda: b_copy(t, 2).start())
        pl.when(z != last)(lambda: b_copy(t, 1).start())
        pl.when(z != 0)(lambda: b_copy(t, last).start())

    def relay_sum(t):
        if not relay:
            return

        @pl.when(inside)
        def _():
            f_copy(t).wait_recv()
            to = outer_peer(2)
            p_buf[t, to] = (
                p_buf[t, to].astype(jnp.float32) + f_buf[t].astype(jnp.float32)
            ).astype(jnp.bfloat16)
            b_copy(t, 2).start()

    def collect(t, i):
        b_copy(t, i).wait_recv()
        acc[...] += q_buf[t, lax.rem(z + outer - i, outer)].astype(jnp.float32)

    def middle(t):
        acc[...] = p_buf[t, z].astype(jnp.float32)
        if relay:
            pl.when(z != 0)(lambda: collect(t, 1))
            pl.when(z != last)(lambda: collect(t, last))
            collect(t, 2)
        else:
            for i in range(1, outer):
                collect(t, i)
        mixed = jnp.dot(
            acc[...].astype(jnp.bfloat16), mix_buf[t], preferred_element_type=jnp.float32
        )
        m_buf[t, z] = mixed.astype(jnp.bfloat16)
        if relay:
            c_copy(t, 2).start()
            pl.when(z != last)(lambda: c_copy(t, 1).start())
            pl.when(z != 0)(lambda: c_copy(t, last).start())
        else:
            for i in range(1, outer):
                c_copy(t, i).start()

    def relay_out(t):
        if not relay:
            return

        @pl.when(inside)
        def _():
            c_copy(t, 2).wait_recv()
            g_copy(t).start()

    def backward(t):
        if relay:
            pl.when(z != 0)(lambda: c_copy(t, 1).wait_recv())
            pl.when(z != last)(lambda: c_copy(t, last).wait_recv())
            pl.when(at_end)(lambda: c_copy(t, 2).wait_recv())
            pl.when(at_end)(lambda: g_copy(t).wait_recv())
        else:
            for i in range(1, outer):
                c_copy(t, i).wait_recv()
        for first in range(0, outer, 2):
            many = min(2, outer - first)
            pair = jnp.concatenate([m_buf[t, first + u] for u in range(many)], axis=1)
            both = jnp.dot(bwd_buf[...], pair, preferred_element_type=jnp.float32)
            for u in range(many):
                part = both[:, u * width:(u + 1) * width]
                out = part[:rows_all] - pltpu.roll(part[rows_all:], channels, 1) * fwd_sign
                v_buf[t, first + u] = out.astype(jnp.bfloat16)
        for i in range(1, group):
            d_copy(t, i).start()
        own_out(t).start()

    stages = tuple(zip((forward, relay_sum, middle, relay_out, backward), LAG))
    for step in range(steps + max(LAG)):
        for stage, lag in stages:
            if 0 <= step - lag < steps:
                stage(step - lag)

    for t in range(steps):
        own_out(t).wait()
        for i in range(1, group):
            d_copy(t, i).wait()
            a_copy(t, i).wait_send()
        if relay:
            pl.when(at_end)(lambda: f_copy(t).wait_send())
            pl.when(inside)(lambda: g_copy(t).wait_send())
            for copy in (b_copy, c_copy):
                copy(t, 2).wait_send()
                pl.when(z != last)(lambda: copy(t, 1).wait_send())
                pl.when(z != 0)(lambda: copy(t, last).wait_send())
        else:
            for i in range(1, outer):
                b_copy(t, i).wait_send()
                c_copy(t, i).wait_send()


def lat_part(x, weight, layer, forward_lat, backward_lat, devices, group):
    modes, rows, width = x.shape
    outer = devices // group
    steps = modes // devices
    kept = backward_lat.shape[2]
    dma = pltpu.SemaphoreType.DMA
    vmem = pl.BlockSpec(memory_space=pltpu.VMEM)
    hbm = pl.BlockSpec(memory_space=pl.ANY)
    return pl.pallas_call(
        functools.partial(lat_kernel, layer, group, outer, steps, rows, kept, width // 2),
        out_shape=jax.ShapeDtypeStruct(x.shape, jnp.bfloat16),
        in_specs=[vmem, hbm, hbm, hbm],
        out_specs=vmem,
        scratch_shapes=[
            pltpu.VMEM((steps, outer, rows * group, width), jnp.bfloat16),
            pltpu.VMEM((steps, outer, kept, width), jnp.bfloat16),
            pltpu.VMEM((steps, outer, kept, width), jnp.bfloat16),
            pltpu.VMEM((steps, outer, kept, width), jnp.bfloat16),
            pltpu.VMEM((steps, outer, rows * group, width), jnp.bfloat16),
            pltpu.VMEM(forward_lat.shape[1:], jnp.bfloat16),
            pltpu.VMEM(backward_lat.shape[1:], jnp.bfloat16),
            pltpu.VMEM((steps, width // 2, width), jnp.bfloat16),
            pltpu.VMEM((steps, width, width), jnp.bfloat16),
            pltpu.VMEM((steps, kept, width), jnp.bfloat16),
            pltpu.VMEM((kept, width), jnp.float32),
            dma((2, steps)), dma((2, steps)),
            dma((2, steps + 1)), dma((steps,)),
            dma((steps, group)), dma((steps, group)),
            dma((steps, outer)), dma((steps, outer)),
            dma((steps, outer)), dma((steps, outer)),
            dma((steps, group)), dma((steps, group)),
        ],
        compiler_params=pltpu.CompilerParams(collective_id=layer, has_side_effects=True),
        name="lat_part",
    )(x, weight, forward_lat, backward_lat)


def modes_out(flat, x_ref, turn):
    modes, rows, width = x_ref.shape
    channels = width // 2
    for n in range(rows):
        part = flat[n * channels:(n + 1) * channels]
        stacked = jnp.concatenate([part[:, :modes], part[:, modes:]], axis=0)
        turn[pl.ds(n, modes, stride=rows), :] = stacked.T
    x_ref[...] = turn[...].reshape(modes, rows, width).astype(jnp.bfloat16)


def lon_kernel(h_ref, table_ref, x_ref, turn):
    rows, channels, lon_count = h_ref.shape
    flat = jnp.dot(
        h_ref[...].reshape(rows * channels, lon_count), table_ref[...],
        preferred_element_type=jnp.float32,
    )
    modes_out(flat, x_ref, turn)


def field_kernel(layer, with_modes, y_ref, h_ref, back_ref, local_ref, *rest):
    if with_modes:
        table_ref, out_ref, x_ref, turn, turned, pointwise = rest
    else:
        out_ref, turn, turned, pointwise = rest
    modes, rows, width = y_ref.shape
    channels = width // 2
    lon_count = h_ref.shape[2]
    span = pointwise.shape[0] // channels

    @pl.when(pl.program_id(0) == 0)
    def _():
        pointwise[...] = jnp.zeros_like(pointwise)
        mixing = local_ref[layer].astype(jnp.float32).T.astype(jnp.bfloat16)
        for n in range(span):
            own = slice(n * channels, (n + 1) * channels)
            pointwise[own, own] = mixing

    turn[...] = y_ref[...].astype(jnp.float32).reshape(modes * rows, width)
    for n in range(rows):
        across = turn[pl.ds(n, modes, stride=rows), :].T
        turned[n * channels:(n + 1) * channels] = jnp.concatenate(
            [across[:channels], across[channels:]], axis=1
        ).astype(jnp.bfloat16)
    chunk = min(CHUNK, lon_count)
    inner = math.sqrt(2.0 / math.pi)
    for first in range(0, rows, span):
        many = span * channels
        spectrum = turned[first * channels:first * channels + many]
        for column in range(0, lon_count, chunk):
            cells = slice(column, column + chunk)
            total = jnp.dot(
                spectrum, back_ref[:, cells], preferred_element_type=jnp.float32
            ) + jnp.dot(
                pointwise[...], h_ref[first:first + span, :, cells].reshape(many, chunk),
                preferred_element_type=jnp.float32,
            )
            curve = jnp.tanh(total * (inner + (inner * 0.044715) * (total * total)))
            out_ref[first:first + span, :, cells] = (
                (total * (0.5 + 0.5 * curve)).astype(jnp.bfloat16).reshape(span, channels, chunk)
            )
    if with_modes:
        flat = jnp.dot(
            out_ref[...].reshape(rows * channels, lon_count), table_ref[...],
            preferred_element_type=jnp.float32,
        )
        modes_out(flat, x_ref, turn)


def whole_block(array):
    return pl.BlockSpec(array.shape, lambda i: (0,) * array.ndim, pipeline_mode=pl.Buffered(1))


def lon_part(h, table):
    rows, channels, lon_count = h.shape
    modes = table.shape[1] // 2
    width = 2 * channels
    return pl.pallas_call(
        lon_kernel,
        grid=(rows // ROW_BLOCK,),
        out_shape=jax.ShapeDtypeStruct((modes, rows, width), jnp.bfloat16),
        in_specs=[
            pl.BlockSpec((ROW_BLOCK, channels, lon_count), lambda i: (i, 0, 0)),
            whole_block(table),
        ],
        out_specs=pl.BlockSpec((modes, ROW_BLOCK, width), lambda i: (0, i, 0)),
        scratch_shapes=[pltpu.VMEM((modes * ROW_BLOCK, width), jnp.float32)],
        name="lon_part",
    )(h, table)


def field_part(y, h, back, local, layer, table=None):
    rows, channels, lon_count = h.shape
    modes, _, width = y.shape
    field = pl.BlockSpec((ROW_BLOCK, channels, lon_count), lambda i: (i, 0, 0))
    spectral = pl.BlockSpec((modes, ROW_BLOCK, width), lambda i: (0, i, 0))
    with_modes = table is not None
    many = max(1, min(ROW_BLOCK, 256 // channels)) * channels
    operands = [y, h, back, local] + ([table] if with_modes else [])
    shapes = [jax.ShapeDtypeStruct(h.shape, jnp.bfloat16)]
    if with_modes:
        shapes.append(jax.ShapeDtypeStruct(y.shape, jnp.bfloat16))
    out = pl.pallas_call(
        functools.partial(field_kernel, layer, with_modes),
        grid=(rows // ROW_BLOCK,),
        out_shape=shapes,
        in_specs=[spectral, field] + [whole_block(a) for a in operands[2:]],
        out_specs=[field, spectral][:len(shapes)],
        scratch_shapes=[
            pltpu.VMEM((modes * ROW_BLOCK, width), jnp.float32),
            pltpu.VMEM((ROW_BLOCK * channels, 2 * modes), jnp.bfloat16),
            pltpu.VMEM((many, many), jnp.bfloat16),
        ],
        name="field_part",
    )(*operands)
    return (out[0], out[1]) if with_modes else (out[0], None)


def shards(fields, spectral_weight, local_weight):
    row_count, channels, lon_count = fields.shape
    layer_count, mode_rows = spectral_weight.shape[:2]
    devices = lax.axis_size("lat")
    group = math.gcd(devices, 8)
    table = lon_table(lon_count, mode_rows)
    forward_lon = jnp.asarray(
        (table / math.sqrt(lon_count)).reshape(lon_count, 2 * mode_rows), jnp.bfloat16
    )
    backward_lon = jnp.asarray(
        (table.transpose(1, 2, 0) / math.sqrt(mode_rows)).reshape(2 * mode_rows, lon_count),
        jnp.bfloat16,
    )
    forward_all, backward_all = lat_tables(devices, group, row_count, KY)
    forward_lat = jnp.asarray(forward_all, jnp.bfloat16)
    backward_lat = jnp.asarray(backward_all, jnp.bfloat16)
    current = fields
    x = lon_part(current, forward_lon)
    for layer_idx in range(layer_count):
        y = lat_part(x, spectral_weight, layer_idx, forward_lat, backward_lat, devices, group)
        last_layer = layer_idx == layer_count - 1
        current, x = field_part(
            y, current, backward_lon, local_weight, layer_idx,
            None if last_layer else forward_lon,
        )
    return current


def solution(mesh):
    return jax.shard_map(
        shards,
        mesh=mesh,
        in_specs=(P(("grp", "lat"), None, None), P(), P()),
        out_specs=P(("grp", "lat"), None, None),
        check_vma=False,
    )
```

```python
import functools
import math

import jax
import jax.numpy as jnp
import numpy as np
from jax import lax
from jax.experimental import pallas as pl
from jax.experimental.pallas import tpu as pltpu
from jax.sharding import PartitionSpec as P

KY = 128
MESH = pl.DeviceIdType.MESH
LAG = (0, 1, 3, 4, 6)
ROW_BLOCK = 8
CHUNK = 512


def lon_table(lon_count, mode_count):
    cells = np.arange(lon_count, dtype=np.int64)[:, None]
    modes = np.arange(mode_count, dtype=np.int64)[None, :]
    angle = (2.0 * np.pi / lon_count) * (cells * modes % lon_count)
    return np.stack([np.cos(angle), -np.sin(angle)], axis=1)


def lat_tables(devices, group, row_count, kept):
    lat_count = devices * row_count
    outer = devices // group
    index = np.arange(kept, dtype=np.int64)
    waves = np.where(index < kept // 2, index, lat_count - kept + index)
    device = np.arange(outer)[:, None, None] * group + np.arange(group)[None, :, None]
    latitudes = (np.arange(row_count)[None, None, :] * devices + device).reshape(outer, -1)
    angle = (2.0 * np.pi / lat_count) * (waves[None, :, None] * latitudes[:, None, :] % lat_count)
    both = np.concatenate([np.cos(angle), np.sin(angle)], axis=1) / math.sqrt(lat_count)
    turned = angle.transpose(0, 2, 1)
    back = np.concatenate([np.cos(turned), np.sin(turned)], axis=1) / math.sqrt(kept)
    return both, back


def lat_kernel(
    layer, group, outer, steps, rows, kept, channels,
    x_ref, weight_ref, fwd_ref, bwd_ref, y_ref,
    r_buf, p_buf, q_buf, m_buf, v_buf, fwd_buf, bwd_buf, w_buf, mix_buf, f_buf, acc, f_sem, g_sem,
    local_sem, w_sem, a_send, a_recv, b_send, b_recv, c_send, c_recv, d_send, d_recv,
):
    me = lax.axis_index("lat")
    z = me // group
    s = lax.rem(me, group)
    rows_all = rows * group

    def inner_peer(i):
        return lax.rem(s + i, group)

    def outer_peer(i):
        return lax.rem(z + i, outer)

    barrier = pltpu.get_barrier_semaphore()
    for i in range(1, group):
        pl.semaphore_signal(
            barrier, inc=1, device_id={"lat": z * group + inner_peer(i)}, device_id_type=MESH
        )
    for i in range(1, outer):
        pl.semaphore_signal(
            barrier, inc=1, device_id={"lat": outer_peer(i) * group + s}, device_id_type=MESH
        )

    def block(who):
        return pl.ds(pl.multiple_of(who * rows, 8), rows)

    def a_copy(t, i):
        to = inner_peer(i)
        return pltpu.make_async_remote_copy(
            src_ref=x_ref.at[pl.ds((to * steps + t) * outer, outer)],
            dst_ref=r_buf.at[t, :, block(s)],
            send_sem=a_send.at[t, i], recv_sem=a_recv.at[t, i],
            device_id={"lat": z * group + to}, device_id_type=MESH,
        )

    def b_copy(t, i):
        to = outer_peer(i)
        return pltpu.make_async_remote_copy(
            src_ref=p_buf.at[t, to], dst_ref=q_buf.at[t, z],
            send_sem=b_send.at[t, i], recv_sem=b_recv.at[t, i],
            device_id={"lat": to * group + s}, device_id_type=MESH,
        )

    def c_copy(t, i):
        to = outer_peer(i)
        return pltpu.make_async_remote_copy(
            src_ref=m_buf.at[t, z], dst_ref=m_buf.at[t, z],
            send_sem=c_send.at[t, i], recv_sem=c_recv.at[t, i],
            device_id={"lat": to * group + s}, device_id_type=MESH,
        )

    def d_copy(t, i):
        to = inner_peer(i)
        return pltpu.make_async_remote_copy(
            src_ref=v_buf.at[t, :, block(to)],
            dst_ref=y_ref.at[pl.ds((s * steps + t) * outer, outer)],
            send_sem=d_send.at[t, i], recv_sem=d_recv.at[t, i],
            device_id={"lat": z * group + to}, device_id_type=MESH,
        )

    def own_in(t):
        return pltpu.make_async_copy(
            x_ref.at[pl.ds((s * steps + t) * outer, outer)], r_buf.at[t, :, block(s)],
            local_sem.at[0, t],
        )

    def own_out(t):
        return pltpu.make_async_copy(
            v_buf.at[t, :, block(s)], y_ref.at[pl.ds((s * steps + t) * outer, outer)],
            local_sem.at[1, t],
        )

    def f_copy(t):
        return pltpu.make_async_remote_copy(
            src_ref=p_buf.at[t, outer - 1 - z], dst_ref=f_buf.at[t],
            send_sem=f_sem.at[0, t], recv_sem=f_sem.at[1, t],
            device_id={"lat": jnp.where(z == 0, 1, outer - 2) * group + s}, device_id_type=MESH,
        )

    def g_copy(t):
        block_of = outer_peer(2)
        return pltpu.make_async_remote_copy(
            src_ref=m_buf.at[t, block_of], dst_ref=m_buf.at[t, block_of],
            send_sem=g_sem.at[0, t], recv_sem=g_sem.at[1, t],
            device_id={"lat": (outer - 1 - block_of) * group + s}, device_id_type=MESH,
        )

    relay = outer == 4
    last = outer - 1
    at_end = jnp.logical_or(z == 0, z == last)
    inside = jnp.logical_not(at_end)

    fwd_copy = pltpu.make_async_copy(fwd_ref.at[z], fwd_buf, local_sem.at[0, steps])
    bwd_copy = pltpu.make_async_copy(bwd_ref.at[z], bwd_buf, local_sem.at[1, steps])
    w_copies = [
        pltpu.make_async_copy(
            weight_ref.at[layer, (s * steps + t) * outer + z], w_buf.at[t], w_sem.at[t]
        )
        for t in range(steps)
    ]
    fwd_copy.start()
    bwd_copy.start()
    for copy in w_copies:
        copy.start()
    for t in range(steps):
        own_in(t).start()
    pl.semaphore_wait(barrier, group - 1 + outer - 1)
    for t in range(steps):
        for i in range(1, group):
            a_copy(t, i).start()
    fwd_copy.wait()
    bwd_copy.wait()

    lane = lax.broadcasted_iota(jnp.int32, (1, 2 * channels), 1)
    fwd_sign = jnp.where(lane < channels, 1.0, -1.0).astype(jnp.float32)
    width = 2 * channels
    for t in range(steps):
        w_copies[t].wait()
        weight = w_buf[t].astype(jnp.float32)
        mix_buf[t, :channels] = w_buf[t]
        mix_buf[t, channels:] = (
            pltpu.roll(weight, channels, 1) * -fwd_sign
        ).astype(jnp.bfloat16)

    def forward(t):
        own_in(t).wait()
        for i in range(1, group):
            a_copy(t, i).wait_recv()
        for first in range(0, outer, 2):
            many = min(2, outer - first)
            pair = jnp.concatenate([r_buf[t, first + u] for u in range(many)], axis=1)
            both = jnp.dot(fwd_buf[...], pair, preferred_element_type=jnp.float32)
            for u in range(many):
                part = both[:, u * width:(u + 1) * width]
                out = part[:kept] + pltpu.roll(part[kept:], channels, 1) * fwd_sign
                p_buf[t, first + u] = out.astype(jnp.bfloat16)
        if not relay:
            for i in range(1, outer):
                b_copy(t, i).start()
            return
        pl.when(at_end)(lambda: f_copy(t).start())
        pl.when(at_end)(lambda: b_copy(t, 2).start())
        pl.when(z != last)(lambda: b_copy(t, 1).start())
        pl.when(z != 0)(lambda: b_copy(t, last).start())

    def relay_sum(t):
        if not relay:
            return

        @pl.when(inside)
        def _():
            f_copy(t).wait_recv()
            to = outer_peer(2)
            p_buf[t, to] = (
                p_buf[t, to].astype(jnp.float32) + f_buf[t].astype(jnp.float32)
            ).astype(jnp.bfloat16)
            b_copy(t, 2).start()

    def collect(t, i):
        b_copy(t, i).wait_recv()
        acc[...] += q_buf[t, lax.rem(z + outer - i, outer)].astype(jnp.float32)

    def middle(t):
        acc[...] = p_buf[t, z].astype(jnp.float32)
        if relay:
            pl.when(z != 0)(lambda: collect(t, 1))
            pl.when(z != last)(lambda: collect(t, last))
            collect(t, 2)
        else:
            for i in range(1, outer):
                collect(t, i)
        mixed = jnp.dot(
            acc[...].astype(jnp.bfloat16), mix_buf[t], preferred_element_type=jnp.float32
        )
        m_buf[t, z] = mixed.astype(jnp.bfloat16)
        if relay:
            c_copy(t, 2).start()
            pl.when(z != last)(lambda: c_copy(t, 1).start())
            pl.when(z != 0)(lambda: c_copy(t, last).start())
        else:
            for i in range(1, outer):
                c_copy(t, i).start()

    def relay_out(t):
        if not relay:
            return

        @pl.when(inside)
        def _():
            c_copy(t, 2).wait_recv()
            g_copy(t).start()

    def backward(t):
        if relay:
            pl.when(z != 0)(lambda: c_copy(t, 1).wait_recv())
            pl.when(z != last)(lambda: c_copy(t, last).wait_recv())
            pl.when(at_end)(lambda: c_copy(t, 2).wait_recv())
            pl.when(at_end)(lambda: g_copy(t).wait_recv())
        else:
            for i in range(1, outer):
                c_copy(t, i).wait_recv()
        for first in range(0, outer, 2):
            many = min(2, outer - first)
            pair = jnp.concatenate([m_buf[t, first + u] for u in range(many)], axis=1)
            both = jnp.dot(bwd_buf[...], pair, preferred_element_type=jnp.float32)
            for u in range(many):
                part = both[:, u * width:(u + 1) * width]
                out = part[:rows_all] - pltpu.roll(part[rows_all:], channels, 1) * fwd_sign
                v_buf[t, first + u] = out.astype(jnp.bfloat16)
        for i in range(1, group):
            d_copy(t, i).start()
        own_out(t).start()

    stages = tuple(zip((forward, relay_sum, middle, relay_out, backward), LAG))
    for step in range(steps + max(LAG)):
        for stage, lag in stages:
            if 0 <= step - lag < steps:
                stage(step - lag)

    for t in range(steps):
        own_out(t).wait()
        for i in range(1, group):
            d_copy(t, i).wait()
            a_copy(t, i).wait_send()
        if relay:
            pl.when(at_end)(lambda: f_copy(t).wait_send())
            pl.when(inside)(lambda: g_copy(t).wait_send())
            for copy in (b_copy, c_copy):
                copy(t, 2).wait_send()
                pl.when(z != last)(lambda: copy(t, 1).wait_send())
                pl.when(z != 0)(lambda: copy(t, last).wait_send())
        else:
            for i in range(1, outer):
                b_copy(t, i).wait_send()
                c_copy(t, i).wait_send()


def lat_part(x, weight, layer, forward_lat, backward_lat, devices, group):
    modes, rows, width = x.shape
    outer = devices // group
    steps = modes // devices
    kept = backward_lat.shape[2]
    dma = pltpu.SemaphoreType.DMA
    vmem = pl.BlockSpec(memory_space=pltpu.VMEM)
    hbm = pl.BlockSpec(memory_space=pl.ANY)
    return pl.pallas_call(
        functools.partial(lat_kernel, layer, group, outer, steps, rows, kept, width // 2),
        out_shape=jax.ShapeDtypeStruct(x.shape, jnp.bfloat16),
        in_specs=[vmem, hbm, hbm, hbm],
        out_specs=vmem,
        scratch_shapes=[
            pltpu.VMEM((steps, outer, rows * group, width), jnp.bfloat16),
            pltpu.VMEM((steps, outer, kept, width), jnp.bfloat16),
            pltpu.VMEM((steps, outer, kept, width), jnp.bfloat16),
            pltpu.VMEM((steps, outer, kept, width), jnp.bfloat16),
            pltpu.VMEM((steps, outer, rows * group, width), jnp.bfloat16),
            pltpu.VMEM(forward_lat.shape[1:], jnp.bfloat16),
            pltpu.VMEM(backward_lat.shape[1:], jnp.bfloat16),
            pltpu.VMEM((steps, width // 2, width), jnp.bfloat16),
            pltpu.VMEM((steps, width, width), jnp.bfloat16),
            pltpu.VMEM((steps, kept, width), jnp.bfloat16),
            pltpu.VMEM((kept, width), jnp.float32),
            dma((2, steps)), dma((2, steps)),
            dma((2, steps + 1)), dma((steps,)),
            dma((steps, group)), dma((steps, group)),
            dma((steps, outer)), dma((steps, outer)),
            dma((steps, outer)), dma((steps, outer)),
            dma((steps, group)), dma((steps, group)),
        ],
        compiler_params=pltpu.CompilerParams(collective_id=layer, has_side_effects=True),
        name="lat_part",
    )(x, weight, forward_lat, backward_lat)


def modes_out(flat, x_ref, turn):
    modes, rows, width = x_ref.shape
    channels = width // 2
    for n in range(rows):
        part = flat[n * channels:(n + 1) * channels]
        stacked = jnp.concatenate([part[:, :modes], part[:, modes:]], axis=0)
        turn[pl.ds(n, modes, stride=rows), :] = stacked.T
    x_ref[...] = turn[...].reshape(modes, rows, width).astype(jnp.bfloat16)


def lon_kernel(h_ref, table_ref, x_ref, turn):
    rows, channels, lon_count = h_ref.shape
    flat = jnp.dot(
        h_ref[...].reshape(rows * channels, lon_count), table_ref[...],
        preferred_element_type=jnp.float32,
    )
    modes_out(flat, x_ref, turn)


def field_kernel(layer, with_modes, y_ref, h_ref, back_ref, local_ref, *rest):
    if with_modes:
        table_ref, out_ref, x_ref, turn, turned, pointwise = rest
    else:
        out_ref, turn, turned, pointwise = rest
    modes, rows, width = y_ref.shape
    channels = width // 2
    lon_count = h_ref.shape[2]
    span = pointwise.shape[0] // channels

    @pl.when(pl.program_id(0) == 0)
    def _():
        pointwise[...] = jnp.zeros_like(pointwise)
        mixing = local_ref[layer].astype(jnp.float32).T.astype(jnp.bfloat16)
        for n in range(span):
            own = slice(n * channels, (n + 1) * channels)
            pointwise[own, own] = mixing

    turn[...] = y_ref[...].astype(jnp.float32).reshape(modes * rows, width)
    for n in range(rows):
        across = turn[pl.ds(n, modes, stride=rows), :].T
        turned[n * channels:(n + 1) * channels] = jnp.concatenate(
            [across[:channels], across[channels:]], axis=1
        ).astype(jnp.bfloat16)
    chunk = min(CHUNK, lon_count)
    inner = math.sqrt(2.0 / math.pi)
    for first in range(0, rows, span):
        many = span * channels
        spectrum = turned[first * channels:first * channels + many]
        for column in range(0, lon_count, chunk):
            cells = slice(column, column + chunk)
            total = jnp.dot(
                spectrum, back_ref[:, cells], preferred_element_type=jnp.float32
            ) + jnp.dot(
                pointwise[...], h_ref[first:first + span, :, cells].reshape(many, chunk),
                preferred_element_type=jnp.float32,
            )
            total = total.astype(jnp.bfloat16)
            curve = jnp.tanh(total * (inner + (inner * 0.044715) * (total * total)))
            out_ref[first:first + span, :, cells] = (
                (total * (0.5 + 0.5 * curve)).reshape(span, channels, chunk)
            )
    if with_modes:
        flat = jnp.dot(
            out_ref[...].reshape(rows * channels, lon_count), table_ref[...],
            preferred_element_type=jnp.float32,
        )
        modes_out(flat, x_ref, turn)


def whole_block(array):
    return pl.BlockSpec(array.shape, lambda i: (0,) * array.ndim, pipeline_mode=pl.Buffered(1))


def lon_part(h, table):
    rows, channels, lon_count = h.shape
    modes = table.shape[1] // 2
    width = 2 * channels
    return pl.pallas_call(
        lon_kernel,
        grid=(rows // ROW_BLOCK,),
        out_shape=jax.ShapeDtypeStruct((modes, rows, width), jnp.bfloat16),
        in_specs=[
            pl.BlockSpec((ROW_BLOCK, channels, lon_count), lambda i: (i, 0, 0)),
            whole_block(table),
        ],
        out_specs=pl.BlockSpec((modes, ROW_BLOCK, width), lambda i: (0, i, 0)),
        scratch_shapes=[pltpu.VMEM((modes * ROW_BLOCK, width), jnp.float32)],
        name="lon_part",
    )(h, table)


def field_part(y, h, back, local, layer, table=None):
    rows, channels, lon_count = h.shape
    modes, _, width = y.shape
    field = pl.BlockSpec((ROW_BLOCK, channels, lon_count), lambda i: (i, 0, 0))
    spectral = pl.BlockSpec((modes, ROW_BLOCK, width), lambda i: (0, i, 0))
    with_modes = table is not None
    many = max(1, min(ROW_BLOCK, 256 // channels)) * channels
    operands = [y, h, back, local] + ([table] if with_modes else [])
    shapes = [jax.ShapeDtypeStruct(h.shape, jnp.bfloat16)]
    if with_modes:
        shapes.append(jax.ShapeDtypeStruct(y.shape, jnp.bfloat16))
    out = pl.pallas_call(
        functools.partial(field_kernel, layer, with_modes),
        grid=(rows // ROW_BLOCK,),
        out_shape=shapes,
        in_specs=[spectral, field] + [whole_block(a) for a in operands[2:]],
        out_specs=[field, spectral][:len(shapes)],
        scratch_shapes=[
            pltpu.VMEM((modes * ROW_BLOCK, width), jnp.float32),
            pltpu.VMEM((ROW_BLOCK * channels, 2 * modes), jnp.bfloat16),
            pltpu.VMEM((many, many), jnp.bfloat16),
        ],
        name="field_part",
    )(*operands)
    return (out[0], out[1]) if with_modes else (out[0], None)


def shards(fields, spectral_weight, local_weight):
    row_count, channels, lon_count = fields.shape
    layer_count, mode_rows = spectral_weight.shape[:2]
    devices = lax.axis_size("lat")
    group = math.gcd(devices, 8)
    table = lon_table(lon_count, mode_rows)
    forward_lon = jnp.asarray(
        (table / math.sqrt(lon_count)).reshape(lon_count, 2 * mode_rows), jnp.bfloat16
    )
    backward_lon = jnp.asarray(
        (table.transpose(1, 2, 0) / math.sqrt(mode_rows)).reshape(2 * mode_rows, lon_count),
        jnp.bfloat16,
    )
    forward_all, backward_all = lat_tables(devices, group, row_count, KY)
    forward_lat = jnp.asarray(forward_all, jnp.bfloat16)
    backward_lat = jnp.asarray(backward_all, jnp.bfloat16)
    current = fields
    x = lon_part(current, forward_lon)
    for layer_idx in range(layer_count):
        y = lat_part(x, spectral_weight, layer_idx, forward_lat, backward_lat, devices, group)
        last_layer = layer_idx == layer_count - 1
        current, x = field_part(
            y, current, backward_lon, local_weight, layer_idx,
            None if last_layer else forward_lon,
        )
    return current


def solution(mesh):
    return jax.shard_map(
        shards,
        mesh=mesh,
        in_specs=(P(("grp", "lat"), None, None), P(), P()),
        out_specs=P(("grp", "lat"), None, None),
        check_vma=False,
    )
```

```python
import functools
import math

import jax
import jax.numpy as jnp
import numpy as np
from jax import lax
from jax.experimental import pallas as pl
from jax.experimental.pallas import tpu as pltpu
from jax.sharding import PartitionSpec as P

KY = 128
MESH = pl.DeviceIdType.MESH
LAG = (0, 1, 4, 5, 8)
ROW_BLOCK = 8
CHUNK = 512


def lon_table(lon_count, mode_count):
    cells = np.arange(lon_count, dtype=np.int64)[:, None]
    modes = np.arange(mode_count, dtype=np.int64)[None, :]
    angle = (2.0 * np.pi / lon_count) * (cells * modes % lon_count)
    return np.stack([np.cos(angle), -np.sin(angle)], axis=1)


def lat_tables(devices, group, row_count, kept):
    lat_count = devices * row_count
    outer = devices // group
    index = np.arange(kept, dtype=np.int64)
    waves = np.where(index < kept // 2, index, lat_count - kept + index)
    device = np.arange(outer)[:, None, None] * group + np.arange(group)[None, :, None]
    latitudes = (np.arange(row_count)[None, None, :] * devices + device).reshape(outer, -1)
    angle = (2.0 * np.pi / lat_count) * (waves[None, :, None] * latitudes[:, None, :] % lat_count)
    both = np.concatenate([np.cos(angle), np.sin(angle)], axis=1) / math.sqrt(lat_count)
    turned = angle.transpose(0, 2, 1)
    back = np.concatenate([np.cos(turned), np.sin(turned)], axis=1) / math.sqrt(kept)
    return both, back


def lat_kernel(
    layer, group, outer, steps, rows, kept, channels,
    x_ref, weight_ref, fwd_ref, bwd_ref, y_ref,
    r_buf, p_buf, q_buf, m_buf, v_buf, fwd_buf, bwd_buf, w_buf, mix_buf, f_buf, acc, f_sem, g_sem,
    local_sem, w_sem, a_send, a_recv, b_send, b_recv, c_send, c_recv, d_send, d_recv,
):
    me = lax.axis_index("lat")
    z = me // group
    s = lax.rem(me, group)
    rows_all = rows * group

    def inner_peer(i):
        return lax.rem(s + i, group)

    def outer_peer(i):
        return lax.rem(z + i, outer)

    barrier = pltpu.get_barrier_semaphore()
    for i in range(1, group):
        pl.semaphore_signal(
            barrier, inc=1, device_id={"lat": z * group + inner_peer(i)}, device_id_type=MESH
        )
    for i in range(1, outer):
        pl.semaphore_signal(
            barrier, inc=1, device_id={"lat": outer_peer(i) * group + s}, device_id_type=MESH
        )

    def block(who):
        return pl.ds(pl.multiple_of(who * rows, 8), rows)

    def a_copy(t, i):
        to = inner_peer(i)
        return pltpu.make_async_remote_copy(
            src_ref=x_ref.at[pl.ds((to * steps + t) * outer, outer)],
            dst_ref=r_buf.at[t, :, block(s)],
            send_sem=a_send.at[t, i], recv_sem=a_recv.at[t, i],
            device_id={"lat": z * group + to}, device_id_type=MESH,
        )

    def b_copy(t, i):
        to = outer_peer(i)
        return pltpu.make_async_remote_copy(
            src_ref=p_buf.at[t, to], dst_ref=q_buf.at[t, z],
            send_sem=b_send.at[t, i], recv_sem=b_recv.at[t, i],
            device_id={"lat": to * group + s}, device_id_type=MESH,
        )

    def c_copy(t, i):
        to = outer_peer(i)
        return pltpu.make_async_remote_copy(
            src_ref=m_buf.at[t, z], dst_ref=m_buf.at[t, z],
            send_sem=c_send.at[t, i], recv_sem=c_recv.at[t, i],
            device_id={"lat": to * group + s}, device_id_type=MESH,
        )

    def d_copy(t, i):
        to = inner_peer(i)
        return pltpu.make_async_remote_copy(
            src_ref=v_buf.at[t, :, block(to)],
            dst_ref=y_ref.at[pl.ds((s * steps + t) * outer, outer)],
            send_sem=d_send.at[t, i], recv_sem=d_recv.at[t, i],
            device_id={"lat": z * group + to}, device_id_type=MESH,
        )

    def own_in(t):
        return pltpu.make_async_copy(
            x_ref.at[pl.ds((s * steps + t) * outer, outer)], r_buf.at[t, :, block(s)],
            local_sem.at[0, t],
        )

    def own_out(t):
        return pltpu.make_async_copy(
            v_buf.at[t, :, block(s)], y_ref.at[pl.ds((s * steps + t) * outer, outer)],
            local_sem.at[1, t],
        )

    def f_copy(t):
        return pltpu.make_async_remote_copy(
            src_ref=p_buf.at[t, outer - 1 - z], dst_ref=f_buf.at[t],
            send_sem=f_sem.at[0, t], recv_sem=f_sem.at[1, t],
            device_id={"lat": jnp.where(z == 0, 1, outer - 2) * group + s}, device_id_type=MESH,
        )

    def g_copy(t):
        block_of = outer_peer(2)
        return pltpu.make_async_remote_copy(
            src_ref=m_buf.at[t, block_of], dst_ref=m_buf.at[t, block_of],
            send_sem=g_sem.at[0, t], recv_sem=g_sem.at[1, t],
            device_id={"lat": (outer - 1 - block_of) * group + s}, device_id_type=MESH,
        )

    relay = outer == 4
    last = outer - 1
    at_end = jnp.logical_or(z == 0, z == last)
    inside = jnp.logical_not(at_end)

    fwd_copy = pltpu.make_async_copy(fwd_ref.at[z], fwd_buf, local_sem.at[0, steps])
    bwd_copy = pltpu.make_async_copy(bwd_ref.at[z], bwd_buf, local_sem.at[1, steps])
    w_copies = [
        pltpu.make_async_copy(
            weight_ref.at[layer, (s * steps + t) * outer + z], w_buf.at[t], w_sem.at[t]
        )
        for t in range(steps)
    ]
    fwd_copy.start()
    bwd_copy.start()
    for copy in w_copies:
        copy.start()
    for t in range(steps):
        own_in(t).start()
    pl.semaphore_wait(barrier, group - 1 + outer - 1)
    for t in range(steps):
        for i in range(1, group):
            a_copy(t, i).start()
    fwd_copy.wait()
    bwd_copy.wait()

    lane = lax.broadcasted_iota(jnp.int32, (1, 2 * channels), 1)
    fwd_sign = jnp.where(lane < channels, 1.0, -1.0).astype(jnp.float32)
    width = 2 * channels
    for t in range(steps):
        w_copies[t].wait()
        weight = w_buf[t].astype(jnp.float32)
        mix_buf[t, :channels] = w_buf[t]
        mix_buf[t, channels:] = (
            pltpu.roll(weight, channels, 1) * -fwd_sign
        ).astype(jnp.bfloat16)

    def forward(t):
        own_in(t).wait()
        for i in range(1, group):
            a_copy(t, i).wait_recv()
        for first in range(0, outer, 2):
            many = min(2, outer - first)
            pair = jnp.concatenate([r_buf[t, first + u] for u in range(many)], axis=1)
            both = jnp.dot(fwd_buf[...], pair, preferred_element_type=jnp.float32)
            for u in range(many):
                part = both[:, u * width:(u + 1) * width]
                out = part[:kept] + pltpu.roll(part[kept:], channels, 1) * fwd_sign
                p_buf[t, first + u] = out.astype(jnp.bfloat16)
        if not relay:
            for i in range(1, outer):
                b_copy(t, i).start()
            return
        pl.when(at_end)(lambda: f_copy(t).start())
        pl.when(at_end)(lambda: b_copy(t, 2).start())
        pl.when(z != last)(lambda: b_copy(t, 1).start())
        pl.when(z != 0)(lambda: b_copy(t, last).start())

    def relay_sum(t):
        if not relay:
            return

        @pl.when(inside)
        def _():
            f_copy(t).wait_recv()
            to = outer_peer(2)
            p_buf[t, to] = (
                p_buf[t, to].astype(jnp.float32) + f_buf[t].astype(jnp.float32)
            ).astype(jnp.bfloat16)
            b_copy(t, 2).start()

    def collect(t, i):
        b_copy(t, i).wait_recv()
        acc[...] += q_buf[t, lax.rem(z + outer - i, outer)].astype(jnp.float32)

    def middle(t):
        acc[...] = p_buf[t, z].astype(jnp.float32)
        if relay:
            pl.when(z != 0)(lambda: collect(t, 1))
            pl.when(z != last)(lambda: collect(t, last))
            collect(t, 2)
        else:
            for i in range(1, outer):
                collect(t, i)
        mixed = jnp.dot(
            acc[...].astype(jnp.bfloat16), mix_buf[t], preferred_element_type=jnp.float32
        )
        m_buf[t, z] = mixed.astype(jnp.bfloat16)
        if relay:
            c_copy(t, 2).start()
            pl.when(z != last)(lambda: c_copy(t, 1).start())
            pl.when(z != 0)(lambda: c_copy(t, last).start())
        else:
            for i in range(1, outer):
                c_copy(t, i).start()

    def relay_out(t):
        if not relay:
            return

        @pl.when(inside)
        def _():
            c_copy(t, 2).wait_recv()
            g_copy(t).start()

    def backward(t):
        if relay:
            pl.when(z != 0)(lambda: c_copy(t, 1).wait_recv())
            pl.when(z != last)(lambda: c_copy(t, last).wait_recv())
            pl.when(at_end)(lambda: c_copy(t, 2).wait_recv())
            pl.when(at_end)(lambda: g_copy(t).wait_recv())
        else:
            for i in range(1, outer):
                c_copy(t, i).wait_recv()
        for first in range(0, outer, 2):
            many = min(2, outer - first)
            pair = jnp.concatenate([m_buf[t, first + u] for u in range(many)], axis=1)
            both = jnp.dot(bwd_buf[...], pair, preferred_element_type=jnp.float32)
            for u in range(many):
                part = both[:, u * width:(u + 1) * width]
                out = part[:rows_all] - pltpu.roll(part[rows_all:], channels, 1) * fwd_sign
                v_buf[t, first + u] = out.astype(jnp.bfloat16)
        for i in range(1, group):
            d_copy(t, i).start()
        own_out(t).start()

    stages = tuple(zip((forward, relay_sum, middle, relay_out, backward), LAG))
    for step in range(steps + max(LAG)):
        for stage, lag in stages:
            if 0 <= step - lag < steps:
                stage(step - lag)

    for t in range(steps):
        own_out(t).wait()
        for i in range(1, group):
            d_copy(t, i).wait()
            a_copy(t, i).wait_send()
        if relay:
            pl.when(at_end)(lambda: f_copy(t).wait_send())
            pl.when(inside)(lambda: g_copy(t).wait_send())
            for copy in (b_copy, c_copy):
                copy(t, 2).wait_send()
                pl.when(z != last)(lambda: copy(t, 1).wait_send())
                pl.when(z != 0)(lambda: copy(t, last).wait_send())
        else:
            for i in range(1, outer):
                b_copy(t, i).wait_send()
                c_copy(t, i).wait_send()


def lat_part(x, weight, layer, forward_lat, backward_lat, devices, group):
    modes, rows, width = x.shape
    outer = devices // group
    steps = modes // devices
    kept = backward_lat.shape[2]
    dma = pltpu.SemaphoreType.DMA
    vmem = pl.BlockSpec(memory_space=pltpu.VMEM)
    hbm = pl.BlockSpec(memory_space=pl.ANY)
    return pl.pallas_call(
        functools.partial(lat_kernel, layer, group, outer, steps, rows, kept, width // 2),
        out_shape=jax.ShapeDtypeStruct(x.shape, jnp.bfloat16),
        in_specs=[vmem, hbm, hbm, hbm],
        out_specs=vmem,
        scratch_shapes=[
            pltpu.VMEM((steps, outer, rows * group, width), jnp.bfloat16),
            pltpu.VMEM((steps, outer, kept, width), jnp.bfloat16),
            pltpu.VMEM((steps, outer, kept, width), jnp.bfloat16),
            pltpu.VMEM((steps, outer, kept, width), jnp.bfloat16),
            pltpu.VMEM((steps, outer, rows * group, width), jnp.bfloat16),
            pltpu.VMEM(forward_lat.shape[1:], jnp.bfloat16),
            pltpu.VMEM(backward_lat.shape[1:], jnp.bfloat16),
            pltpu.VMEM((steps, width // 2, width), jnp.bfloat16),
            pltpu.VMEM((steps, width, width), jnp.bfloat16),
            pltpu.VMEM((steps, kept, width), jnp.bfloat16),
            pltpu.VMEM((kept, width), jnp.float32),
            dma((2, steps)), dma((2, steps)),
            dma((2, steps + 1)), dma((steps,)),
            dma((steps, group)), dma((steps, group)),
            dma((steps, outer)), dma((steps, outer)),
            dma((steps, outer)), dma((steps, outer)),
            dma((steps, group)), dma((steps, group)),
        ],
        compiler_params=pltpu.CompilerParams(collective_id=layer, has_side_effects=True),
        name="lat_part",
    )(x, weight, forward_lat, backward_lat)


def modes_out(flat, x_ref, turn):
    modes, rows, width = x_ref.shape
    channels = width // 2
    for n in range(rows):
        part = flat[n * channels:(n + 1) * channels]
        stacked = jnp.concatenate([part[:, :modes], part[:, modes:]], axis=0)
        turn[pl.ds(n, modes, stride=rows), :] = stacked.T
    x_ref[...] = turn[...].reshape(modes, rows, width).astype(jnp.bfloat16)


def lon_kernel(h_ref, table_ref, x_ref, turn):
    rows, channels, lon_count = h_ref.shape
    flat = jnp.dot(
        h_ref[...].reshape(rows * channels, lon_count), table_ref[...],
        preferred_element_type=jnp.float32,
    )
    modes_out(flat, x_ref, turn)


def field_kernel(layer, with_modes, y_ref, h_ref, back_ref, local_ref, *rest):
    if with_modes:
        table_ref, out_ref, x_ref, turn, turned, pointwise = rest
    else:
        out_ref, turn, turned, pointwise = rest
    modes, rows, width = y_ref.shape
    channels = width // 2
    lon_count = h_ref.shape[2]
    span = pointwise.shape[0] // channels

    @pl.when(pl.program_id(0) == 0)
    def _():
        pointwise[...] = jnp.zeros_like(pointwise)
        mixing = local_ref[layer].astype(jnp.float32).T.astype(jnp.bfloat16)
        for n in range(span):
            own = slice(n * channels, (n + 1) * channels)
            pointwise[own, own] = mixing

    turn[...] = y_ref[...].astype(jnp.float32).reshape(modes * rows, width)
    for n in range(rows):
        across = turn[pl.ds(n, modes, stride=rows), :].T
        turned[n * channels:(n + 1) * channels] = jnp.concatenate(
            [across[:channels], across[channels:]], axis=1
        ).astype(jnp.bfloat16)
    chunk = min(CHUNK, lon_count)
    inner = math.sqrt(2.0 / math.pi)
    for first in range(0, rows, span):
        many = span * channels
        spectrum = turned[first * channels:first * channels + many]
        for column in range(0, lon_count, chunk):
            cells = slice(column, column + chunk)
            total = jnp.dot(
                spectrum, back_ref[:, cells], preferred_element_type=jnp.float32
            ) + jnp.dot(
                pointwise[...], h_ref[first:first + span, :, cells].reshape(many, chunk),
                preferred_element_type=jnp.float32,
            )
            total = total.astype(jnp.bfloat16)
            curve = jnp.tanh(total * (inner + (inner * 0.044715) * (total * total)))
            out_ref[first:first + span, :, cells] = (
                (total * (0.5 + 0.5 * curve)).reshape(span, channels, chunk)
            )
    if with_modes:
        flat = jnp.dot(
            out_ref[...].reshape(rows * channels, lon_count), table_ref[...],
            preferred_element_type=jnp.float32,
        )
        modes_out(flat, x_ref, turn)


def whole_block(array):
    return pl.BlockSpec(array.shape, lambda i: (0,) * array.ndim, pipeline_mode=pl.Buffered(1))


def lon_part(h, table):
    rows, channels, lon_count = h.shape
    modes = table.shape[1] // 2
    width = 2 * channels
    return pl.pallas_call(
        lon_kernel,
        grid=(rows // ROW_BLOCK,),
        out_shape=jax.ShapeDtypeStruct((modes, rows, width), jnp.bfloat16),
        in_specs=[
            pl.BlockSpec((ROW_BLOCK, channels, lon_count), lambda i: (i, 0, 0)),
            whole_block(table),
        ],
        out_specs=pl.BlockSpec((modes, ROW_BLOCK, width), lambda i: (0, i, 0)),
        scratch_shapes=[pltpu.VMEM((modes * ROW_BLOCK, width), jnp.float32)],
        name="lon_part",
    )(h, table)


def field_part(y, h, back, local, layer, table=None):
    rows, channels, lon_count = h.shape
    modes, _, width = y.shape
    field = pl.BlockSpec((ROW_BLOCK, channels, lon_count), lambda i: (i, 0, 0))
    spectral = pl.BlockSpec((modes, ROW_BLOCK, width), lambda i: (0, i, 0))
    with_modes = table is not None
    many = max(1, min(ROW_BLOCK, 256 // channels)) * channels
    operands = [y, h, back, local] + ([table] if with_modes else [])
    shapes = [jax.ShapeDtypeStruct(h.shape, jnp.bfloat16)]
    if with_modes:
        shapes.append(jax.ShapeDtypeStruct(y.shape, jnp.bfloat16))
    out = pl.pallas_call(
        functools.partial(field_kernel, layer, with_modes),
        grid=(rows // ROW_BLOCK,),
        out_shape=shapes,
        in_specs=[spectral, field] + [whole_block(a) for a in operands[2:]],
        out_specs=[field, spectral][:len(shapes)],
        scratch_shapes=[
            pltpu.VMEM((modes * ROW_BLOCK, width), jnp.float32),
            pltpu.VMEM((ROW_BLOCK * channels, 2 * modes), jnp.bfloat16),
            pltpu.VMEM((many, many), jnp.bfloat16),
        ],
        name="field_part",
    )(*operands)
    return (out[0], out[1]) if with_modes else (out[0], None)


def shards(fields, spectral_weight, local_weight):
    row_count, channels, lon_count = fields.shape
    layer_count, mode_rows = spectral_weight.shape[:2]
    devices = lax.axis_size("lat")
    group = math.gcd(devices, 8)
    table = lon_table(lon_count, mode_rows)
    forward_lon = jnp.asarray(
        (table / math.sqrt(lon_count)).reshape(lon_count, 2 * mode_rows), jnp.bfloat16
    )
    backward_lon = jnp.asarray(
        (table.transpose(1, 2, 0) / math.sqrt(mode_rows)).reshape(2 * mode_rows, lon_count),
        jnp.bfloat16,
    )
    forward_all, backward_all = lat_tables(devices, group, row_count, KY)
    forward_lat = jnp.asarray(forward_all, jnp.bfloat16)
    backward_lat = jnp.asarray(backward_all, jnp.bfloat16)
    current = fields
    x = lon_part(current, forward_lon)
    for layer_idx in range(layer_count):
        y = lat_part(x, spectral_weight, layer_idx, forward_lat, backward_lat, devices, group)
        last_layer = layer_idx == layer_count - 1
        current, x = field_part(
            y, current, backward_lon, local_weight, layer_idx,
            None if last_layer else forward_lon,
        )
    return current


def solution(mesh):
    return jax.shard_map(
        shards,
        mesh=mesh,
        in_specs=(P(("grp", "lat"), None, None), P(), P()),
        out_specs=P(("grp", "lat"), None, None),
        check_vma=False,
    )
```
